32 devices in a mesh: dp: 8 (over z, y), tensor: 4 (over x, core).
Axes of the slice: x: 2, y: 2, z: 4, core: 2. Of those that a mesh axis runs over, the one named last changes fastest.
Arguments:
- layer_in: bfloat16 [4096, 1024], P(('dp', 'tensor')), may hold values from -6 to 6
- doc_pos: int32 [4096], P('dp'), may hold values from 0 to 1999, as said below
- gain_attend: float32 [1024], replicated, may hold values from 0.5 to 1.5
- shift_attend: float32 [1024], replicated, may hold values from -3 to 3
- gain_dense: float32 [1024], replicated, may hold values from 0.5 to 1.5
- shift_dense: float32 [1024], replicated, may hold values from -3 to 3
- w_qkv: bfloat16 [1024, 3072], P('dp', 'tensor')
- b_qkv: float32 [3072], P('tensor'), may hold values from -3 to 3
- w_out: bfloat16 [1024, 1024], P('tensor', 'dp'), may hold values from -0.75 to 0.75
- b_out: float32 [1024], replicated, may hold values from -3 to 3
- w_up: bfloat16 [1024, 4096], P('dp', 'tensor'), may hold values from -0.1875 to 0.1875
- b_up: float32 [4096], P('tensor'), may hold values from -3 to 3
- w_down: bfloat16 [4096, 1024], P('tensor', 'dp'), may hold values from -0.09375 to 0.09375
- b_down: float32 [1024], replicated, may hold values from -3 to 3
- grad_out: bfloat16 [4096, 1024], P(('dp', 'tensor')), may hold values from -6 to 6
Outputs:
- layer_out: bfloat16 [4096, 1024], P(('dp', 'tensor'))
- grad_in: float32 [4096, 1024], P(('dp', 'tensor'))
- dgain_attend: float32 [1024], replicated
- dshift_attend: float32 [1024], replicated
- dgain_dense: float32 [1024], replicated
- dshift_dense: float32 [1024], replicated
- dw_qkv: float32 [1024, 3072], P('dp', 'tensor')
- db_qkv: float32 [3072], P('tensor')
- dw_out: float32 [1024, 1024], P('tensor', 'dp')
- db_out: float32 [1024], replicated
- dw_up: float32 [1024, 4096], P('dp', 'tensor')
- db_up: float32 [4096], P('tensor')
- dw_down: float32 [4096, 1024], P('tensor', 'dp')
- db_down: float32 [1024], replicated
The draws below stay inside these ranges and needn't reach their ends.
Inputs may be any that keep to these rules, and one draw needn't show every extreme that they name: `doc_pos`: positions rise by one from token to token and restart at 0 where a document begins; the first token is at position 0; every whole document has 200 to 2000 tokens and one has exactly 2000; the last may be cut short, and a document may run across the border of two packed sequences.
All inputs are finite; a program needn't handle non-finite values.
Results may differ from the reference program's by a relative error of at most 0.02.
The reference program's roundings to bfloat16 on the way (of `first_in`, `queries`, `context`, `hidden`, `dcontext`, `dpreact_b`, `dscores` and `dfused_b`) count: a program that leaves them out, or rounds other values in their place, can miss the bound.
Values may be sent and summed in bfloat16 or wider, within the bound.
No kernel may reach another device: no remote copies, remote signals or barrier semaphores. Data moves between devices by JAX's collectives and lax.ppermute only.
A program may use at most 128 MiB of HBM per device.

```python
import jax
import jax.numpy as jnp
from jax import lax

D = 1024
HEADS = 16
HD = 64
ROT = 16
FF = 4096
SEQ = 4096
DOC_MAX = 2000
DOC_MIN = 200
TOKENS = 4096
NSEQ = 1


def draw_doc_pos(key, part):
    doc_count = TOKENS // DOC_MIN + 2
    lengths = jax.random.randint(jax.random.fold_in(key, 11), (doc_count,), DOC_MIN, DOC_MAX + 1)
    longest = jax.random.randint(jax.random.fold_in(key, 12), (), 0, 2)
    lengths = jnp.where(jnp.arange(doc_count) == longest, DOC_MAX, lengths).astype(jnp.int32)
    doc_ends = jnp.cumsum(lengths).astype(jnp.int32)
    starts = doc_ends - lengths
    places = jnp.arange(TOKENS, dtype=jnp.int32)
    owners = jnp.sum((places[:, None] >= doc_ends[None, :]).astype(jnp.int32), axis=1)
    return (places - jnp.take(starts, owners)).astype(jnp.int32)


def draw_w_qkv(key, part):
    entries = jax.random.truncated_normal(key, -4.0, 4.0, (D, HEADS, 3, HD), jnp.float32) * D ** (-0.5)
    return entries.reshape(D, 3 * D).astype(jnp.bfloat16)


def block_levels(key, dims, shards, low, high):
    gain = 1.0
    for position, blocks in shards:
        draws = jax.random.uniform(jax.random.fold_in(jax.random.fold_in(key, 6), position), (blocks,), jnp.float32, low / len(shards), high / len(shards))
        gain = gain * jnp.repeat(jnp.exp(draws), dims[position] // blocks).reshape((-1,) + (1,) * (len(dims) - 1 - position))
    return gain


def bell_draw(stream_key, extent, scale, most, split=(), kind=jnp.bfloat16):
    drawn = scale * jax.random.normal(stream_key, extent, jnp.float32)
    if split:
        drawn = drawn * block_levels(stream_key, extent, split, -0.22, 0.18)
    return jnp.clip(drawn, -most, most).astype(kind)


def setup_inputs(seed: int = 0) -> dict:
    arg_keys = jax.random.split(jax.random.key(seed), 16)
    layer_in = bell_draw(arg_keys[0], (TOKENS, D), 1.0, 6.0, ((0, 32),))
    doc_pos = draw_doc_pos(jax.random.fold_in(arg_keys[15], 71), 0)
    gain_attend = jnp.clip(1.0 + 0.1 * jax.random.normal(arg_keys[2], (D,), jnp.float32), 0.5, 1.5)
    shift_attend = bell_draw(arg_keys[3], (D,), 0.5, 3.0, (), jnp.float32)
    gain_dense = jnp.clip(1.0 + 0.1 * jax.random.normal(arg_keys[4], (D,), jnp.float32), 0.5, 1.5)
    shift_dense = bell_draw(arg_keys[5], (D,), 0.5, 3.0, (), jnp.float32)
    w_qkv = draw_w_qkv(jax.random.fold_in(arg_keys[15], 71), 0)
    b_qkv = bell_draw(arg_keys[7], (3 * D,), 0.5, 3.0, ((0, 4),), jnp.float32)
    w_out = bell_draw(arg_keys[8], (D, D), (D // 16) ** -0.5, 0.75, ((0, 4), (1, 8)))
    b_out = bell_draw(arg_keys[9], (D,), 0.5, 3.0, (), jnp.float32)
    w_up = bell_draw(arg_keys[10], (D, FF), D ** -0.5, 0.1875, ((0, 8), (1, 4)))
    b_up = bell_draw(arg_keys[11], (FF,), 0.5, 3.0, ((0, 4),), jnp.float32)
    w_down = bell_draw(arg_keys[12], (FF, D), FF ** -0.5, 0.09375, ((0, 4), (1, 8)))
    b_down = bell_draw(arg_keys[13], (D,), 0.5, 3.0, (), jnp.float32)
    grad_out = bell_draw(arg_keys[14], (TOKENS, D), 1.0, 6.0, ((0, 32),))
    return dict(layer_in=layer_in, doc_pos=doc_pos, gain_attend=gain_attend, shift_attend=shift_attend, gain_dense=gain_dense, shift_dense=shift_dense, w_qkv=w_qkv, b_qkv=b_qkv, w_out=w_out, b_out=b_out, w_up=w_up, b_up=b_up, w_down=w_down, b_down=b_down, grad_out=grad_out)


EPS = 1e-05
MASKED = -1e+30

def normalize(x_float):
    average = lax.optimization_barrier(jnp.mean(x_float, axis=-1, keepdims=True))
    centred = x_float - average
    inv_std = lax.rsqrt(lax.optimization_barrier(jnp.mean(centred * centred, axis=-1, keepdims=True)) + EPS)
    return (centred * inv_std, inv_std)

def norm_back(dnormed, normed, inv_std):
    return inv_std * (dnormed - lax.optimization_barrier(jnp.mean(dnormed, axis=-1, keepdims=True)) - normed * lax.optimization_barrier(jnp.mean(dnormed * normed, axis=-1, keepdims=True)))

def rotary_tables(positions):
    half_rot = ROT // 2
    inv_freq = jnp.power(10000.0, -2.0 * jnp.arange(half_rot, dtype=jnp.float32) / ROT)
    angles = positions.astype(jnp.float32)[:, None] * inv_freq[None, :]
    cos_tab = jnp.cos(angles)
    sin_tab = jnp.sin(angles)
    return (jnp.concatenate([cos_tab, cos_tab], axis=-1), jnp.concatenate([sin_tab, sin_tab], axis=-1))

def rotate(vectors, cos_tab, sin_tab):
    half_rot = ROT // 2
    leading = vectors[..., :ROT]
    turned = jnp.concatenate([-leading[..., half_rot:], leading[..., :half_rot]], axis=-1)
    return jnp.concatenate([leading * cos_tab + turned * sin_tab, vectors[..., ROT:]], axis=-1)

def rotate_back(upstream, cos_tab, sin_tab):
    half_rot = ROT // 2
    leading = upstream[..., :ROT]
    shifted = leading * sin_tab
    turned = jnp.concatenate([shifted[..., half_rot:], -shifted[..., :half_rot]], axis=-1)
    return jnp.concatenate([leading * cos_tab + turned, upstream[..., ROT:]], axis=-1)

def gelu_slope(preact):
    return 0.5 * (1.0 + lax.erf(preact * 0.7071067811865476)) + preact * jnp.exp(-0.5 * preact * preact) * 0.3989422804014327

def by_head(tensor3):
    return jnp.transpose(tensor3, (1, 0, 2))

def scores_of(q_head, k_head, allowed):
    raw_scores = jnp.dot(q_head, k_head.T, preferred_element_type=jnp.float32) * HD ** (-0.5)
    return jnp.where(allowed, raw_scores, MASKED)

def reference(layer_in, doc_pos, gain_attend, shift_attend, gain_dense, shift_dense, w_qkv, b_qkv, w_out, b_out, w_up, b_up, w_down, b_down, grad_out):
    indices = jnp.arange(SEQ, dtype=jnp.int32)
    causal = indices[None, :] <= indices[:, None]

    def one_seq(totals, seq_items):
        seq_in, seq_pos, seq_grad = seq_items
        x_float = seq_in.astype(jnp.float32)
        normed, inv_std = normalize(x_float)
        first_in = (normed * gain_attend + shift_attend).astype(jnp.bfloat16)
        second_in = (normed * gain_dense + shift_dense).astype(jnp.bfloat16)
        joined_qkv = (jnp.dot(first_in, w_qkv, preferred_element_type=jnp.float32) + b_qkv).reshape(SEQ, HEADS, 3, HD)
        cos_tab, sin_tab = rotary_tables(seq_pos)
        cos_tab = cos_tab[:, None, :]
        sin_tab = sin_tab[:, None, :]
        queries = rotate(joined_qkv[:, :, 0], cos_tab, sin_tab).astype(jnp.bfloat16)
        keys_rot = rotate(joined_qkv[:, :, 1], cos_tab, sin_tab).astype(jnp.bfloat16)
        values = joined_qkv[:, :, 2].astype(jnp.bfloat16)
        allowed = causal & (indices[:, None] - indices[None, :] <= seq_pos[:, None])

        def head_forward(head_parts):
            q_head, k_head, v_head = head_parts
            scores = scores_of(q_head, k_head, allowed)
            row_peak = lax.optimization_barrier(jnp.max(scores, axis=-1, keepdims=True))
            logsum = row_peak + jnp.log(lax.optimization_barrier(jnp.sum(jnp.exp(scores - row_peak), axis=-1, keepdims=True)))
            softmax = jnp.exp(scores - logsum).astype(jnp.bfloat16)
            return (jnp.dot(softmax, v_head, preferred_element_type=jnp.float32), logsum[:, 0])
        context, logsums = lax.map(head_forward, (by_head(queries), by_head(keys_rot), by_head(values)))
        context = by_head(context).reshape(SEQ, D).astype(jnp.bfloat16)
        preact = jnp.dot(second_in, w_up, preferred_element_type=jnp.float32) + b_up
        hidden = jax.nn.gelu(preact, approximate=False).astype(jnp.bfloat16)
        branch = jnp.dot(context, w_out, preferred_element_type=jnp.float32) + jnp.dot(hidden, w_down, preferred_element_type=jnp.float32)
        seq_out = (x_float + b_out + b_down + branch).astype(jnp.bfloat16)
        grad_float = seq_grad.astype(jnp.float32)
        bias_grad = lax.optimization_barrier(jnp.sum(grad_float, axis=0))
        wout_grad = jnp.dot(context.T, seq_grad, preferred_element_type=jnp.float32)
        wdown_grad = jnp.dot(hidden.T, seq_grad, preferred_element_type=jnp.float32)
        dcontext = jnp.dot(seq_grad, w_out.T, preferred_element_type=jnp.float32).astype(jnp.bfloat16)
        dpreact = jnp.dot(seq_grad, w_down.T, preferred_element_type=jnp.float32) * gelu_slope(preact)
        dpreact_b = dpreact.astype(jnp.bfloat16)
        bup_grad = lax.optimization_barrier(jnp.sum(dpreact, axis=0))
        wup_grad = jnp.dot(second_in.T, dpreact_b, preferred_element_type=jnp.float32)
        dsecond = jnp.dot(dpreact_b, w_up.T, preferred_element_type=jnp.float32)
        dctx_heads = dcontext.reshape(SEQ, HEADS, HD)
        deltas = lax.optimization_barrier(jnp.sum(dctx_heads.astype(jnp.float32) * context.reshape(SEQ, HEADS, HD).astype(jnp.float32), axis=-1))

        def head_backward(head_parts):
            q_head, k_head, v_head, dctx_head, logsum, delta_head = head_parts
            scores = scores_of(q_head, k_head, allowed)
            softmax_f = jnp.exp(scores - logsum[:, None])
            softmax_b = softmax_f.astype(jnp.bfloat16)
            dv_head = jnp.dot(softmax_b.T, dctx_head, preferred_element_type=jnp.float32)
            dsoftmax = jnp.dot(dctx_head, v_head.T, preferred_element_type=jnp.float32)
            dscores = (softmax_f * (dsoftmax - delta_head[:, None]) * HD ** (-0.5)).astype(jnp.bfloat16)
            dq_head = jnp.dot(dscores, k_head, preferred_element_type=jnp.float32)
            dk_head = jnp.dot(dscores.T, q_head, preferred_element_type=jnp.float32)
            return (dq_head, dk_head, dv_head)
        dq_all, dk_all, dv_all = lax.map(head_backward, (by_head(queries), by_head(keys_rot), by_head(values), by_head(dctx_heads), logsums, deltas.T))
        dq_pre = rotate_back(by_head(dq_all), cos_tab, sin_tab)
        dk_pre = rotate_back(by_head(dk_all), cos_tab, sin_tab)
        dfused = jnp.stack([dq_pre, dk_pre, by_head(dv_all)], axis=2).reshape(SEQ, 3 * D)
        bqkv_grad = lax.optimization_barrier(jnp.sum(dfused, axis=0))
        dfused_b = dfused.astype(jnp.bfloat16)
        wqkv_grad = jnp.dot(first_in.T, dfused_b, preferred_element_type=jnp.float32)
        dfirst = jnp.dot(dfused_b, w_qkv.T, preferred_element_type=jnp.float32)
        dnormed = dfirst * gain_attend + dsecond * gain_dense
        seq_dx = grad_float + norm_back(dnormed, normed, inv_std)
        terms = (lax.optimization_barrier(jnp.sum(dfirst * normed, axis=0)), lax.optimization_barrier(jnp.sum(dfirst, axis=0)), lax.optimization_barrier(jnp.sum(dsecond * normed, axis=0)), lax.optimization_barrier(jnp.sum(dsecond, axis=0)), bias_grad, bqkv_grad, bup_grad, wqkv_grad, wout_grad, wup_grad, wdown_grad)
        new_totals = tuple((older + newer for older, newer in zip(totals, terms)))
        return (new_totals, (seq_out, seq_dx))
    vec_zero = jnp.zeros((D,), jnp.float32)
    start_totals = (vec_zero, vec_zero, vec_zero, vec_zero, vec_zero, jnp.zeros((3 * D,), jnp.float32), jnp.zeros((FF,), jnp.float32), jnp.zeros((D, 3 * D), jnp.float32), jnp.zeros((D, D), jnp.float32), jnp.zeros((D, FF), jnp.float32), jnp.zeros((FF, D), jnp.float32))
    totals, outputs = lax.scan(one_seq, start_totals, (layer_in.reshape(NSEQ, SEQ, D), doc_pos.reshape(NSEQ, SEQ), grad_out.reshape(NSEQ, SEQ, D)))
    layer_out = outputs[0].reshape(TOKENS, D)
    grad_in = outputs[1].reshape(TOKENS, D)
    return (layer_out, grad_in, totals[0], totals[1], totals[2], totals[3], totals[7], totals[5], totals[8], totals[4], totals[9], totals[6], totals[10], totals[4])
```

```python
import jax
import jax.numpy as jnp
from jax import lax
from jax.sharding import PartitionSpec as P

HEADS = 16
HD = 64
ROT = 16
SEQ = 4096
DOC_MAX = 2000
EPS = 1e-05
MASKED = -1e30
AXES = ("dp", "tensor")
BF = jnp.bfloat16
F32 = jnp.float32


def exchange(value, by_dp, by_tensor):
    tensor = lax.axis_size("tensor")
    count = lax.axis_size("dp") * tensor
    pairs = [
        (i, ((i // tensor) ^ by_dp) * tensor + ((i % tensor) ^ by_tensor)) for i in range(count)
    ]
    return lax.ppermute(value, AXES, pairs)


def shift_groups(value, by):
    count = lax.axis_size("dp")
    pairs = [(i, i + 2 * by) for i in range(count) if 0 <= i + 2 * by < count]
    return lax.ppermute(value, "dp", pairs)


def column_groups():
    return [[2 * g + y for g in range(lax.axis_size("dp") // 2)] for y in range(2)]


def gather_groups(piece):
    groups = lax.axis_size("dp") // 2
    if groups != 4:
        return lax.all_gather(piece, "dp", axis=0, axis_index_groups=column_groups())
    mine = lax.axis_index("dp") // 2
    whole = jnp.zeros((groups,) + piece.shape, piece.dtype)
    whole = lax.dynamic_update_index_in_dim(whole, piece, mine, 0)
    for k in range(1, groups):
        whole = lax.dynamic_update_index_in_dim(whole, exchange(piece, 2 * k, 0), mine ^ k, 0)
    return whole


def scatter_groups(partials):
    groups = lax.axis_size("dp") // 2
    if groups != 4:
        return lax.psum_scatter(
            partials, "dp", scatter_dimension=0, axis_index_groups=column_groups()
        )
    mine = lax.axis_index("dp") // 2
    narrow = partials.astype(BF)
    total = lax.dynamic_index_in_dim(partials, mine, 0, keepdims=False)
    for k in range(1, groups):
        sent = lax.dynamic_index_in_dim(narrow, mine ^ k, 0, keepdims=False)
        total = total + exchange(sent, 2 * k, 0).astype(F32)
    return total


def sum_groups(vectors):
    groups = lax.axis_size("dp") // 2
    if groups != 4:
        gathered = lax.all_gather(vectors, "dp", axis=0, axis_index_groups=column_groups())
        return jnp.sum(gathered, axis=0)
    vectors = vectors + exchange(vectors, 2, 0)
    return vectors + exchange(vectors, 4, 0)


def gather_rows(rows):
    y = lax.axis_index("dp") % 2
    t = lax.axis_index("tensor")
    x, c = t // 2, t % 2
    four = jnp.zeros((4,) + rows.shape, rows.dtype)
    four = lax.dynamic_update_index_in_dim(four, rows, y * 2 + x, 0)
    four = lax.dynamic_update_index_in_dim(four, exchange(rows, 0, 2), y * 2 + (1 - x), 0)
    four = lax.dynamic_update_index_in_dim(four, exchange(rows, 1, 0), (1 - y) * 2 + x, 0)
    four = lax.dynamic_update_index_in_dim(four, exchange(rows, 1, 2), (1 - y) * 2 + (1 - x), 0)
    other = exchange(four, 0, 1)
    whole = jnp.where(
        c == 0, jnp.stack([four, other], axis=1), jnp.stack([other, four], axis=1)
    )
    return whole.reshape((8 * rows.shape[0],) + rows.shape[1:])


def scatter_rows(partial):
    y = lax.axis_index("dp") % 2
    t = lax.axis_index("tensor")
    x, c = t // 2, t % 2
    rows = partial.shape[0] // 8
    blocks = partial.reshape((4, 2, rows) + partial.shape[1:])
    sent = lax.dynamic_index_in_dim(blocks, 1 - c, 1, keepdims=False).astype(BF)
    four = lax.dynamic_index_in_dim(blocks, c, 1, keepdims=False) + exchange(
        sent, 0, 1
    ).astype(F32)
    narrow = four.astype(BF)
    total = lax.dynamic_index_in_dim(four, y * 2 + x, 0, keepdims=False)
    for by_y, by_x in ((0, 1), (1, 0), (1, 1)):
        piece = lax.dynamic_index_in_dim(narrow, (y ^ by_y) * 2 + (x ^ by_x), 0, keepdims=False)
        total = total + exchange(piece, by_y, 2 * by_x).astype(F32)
    return total


def halves_first(y, mine, other, axis):
    return jnp.where(
        y == 0,
        jnp.concatenate([mine, other], axis=axis),
        jnp.concatenate([other, mine], axis=axis),
    )


def normalize(x_float):
    average = jnp.mean(x_float, axis=-1, keepdims=True)
    centred = x_float - average
    inv_std = lax.rsqrt(jnp.mean(centred * centred, axis=-1, keepdims=True) + EPS)
    return (centred * inv_std, inv_std)


def norm_back(dnormed, normed, inv_std):
    return inv_std * (
        dnormed
        - jnp.mean(dnormed, axis=-1, keepdims=True)
        - normed * jnp.mean(dnormed * normed, axis=-1, keepdims=True)
    )


def rotary_tables(positions):
    half_rot = ROT // 2
    inv_freq = jnp.power(10000.0, -2.0 * jnp.arange(half_rot, dtype=F32) / ROT)
    angles = positions.astype(F32)[:, None] * inv_freq[None, :]
    cos_tab = jnp.cos(angles)
    sin_tab = jnp.sin(angles)
    return (
        jnp.concatenate([cos_tab, cos_tab], axis=-1),
        jnp.concatenate([sin_tab, sin_tab], axis=-1),
    )


def rotate(vectors, cos_tab, sin_tab):
    half_rot = ROT // 2
    leading = vectors[..., :ROT]
    turned = jnp.concatenate([-leading[..., half_rot:], leading[..., :half_rot]], axis=-1)
    return jnp.concatenate([leading * cos_tab + turned * sin_tab, vectors[..., ROT:]], axis=-1)


def rotate_back(upstream, cos_tab, sin_tab):
    half_rot = ROT // 2
    leading = upstream[..., :ROT]
    shifted = leading * sin_tab
    turned = jnp.concatenate([shifted[..., half_rot:], -shifted[..., :half_rot]], axis=-1)
    return jnp.concatenate([leading * cos_tab + turned, upstream[..., ROT:]], axis=-1)


def gelu_slope(preact):
    return (
        0.5 * (1.0 + lax.erf(preact * 0.7071067811865476))
        + preact * jnp.exp(-0.5 * preact * preact) * 0.3989422804014327
    )


def dot_nn(left, right):
    return jnp.dot(left, right, preferred_element_type=F32)


def dot_nt(left, right):
    return lax.dot_general(left, right, (((1,), (1,)), ((), ())), preferred_element_type=F32)


def dot_tn(left, right):
    return lax.dot_general(left, right, (((0,), (0,)), ((), ())), preferred_element_type=F32)


def shards(
    layer_in,
    doc_pos,
    gain_attend,
    shift_attend,
    gain_dense,
    shift_dense,
    w_qkv,
    b_qkv,
    w_out,
    b_out,
    w_up,
    b_up,
    w_down,
    b_down,
    grad_out,
):
    dp = lax.axis_index("dp")
    y = dp % 2
    group = dp // 2
    my_heads = HEADS // lax.axis_size("tensor") // 2
    head_width = my_heads * HD
    score_scale = HD ** (-0.5)
    d_rows = w_qkv.shape[0]
    units = w_up.shape[1] // 2
    d_model = layer_in.shape[1]

    attend_w = jnp.concatenate(
        [
            w_qkv.reshape(d_rows, 2, 3 * head_width).transpose(1, 0, 2),
            w_out.T.reshape(d_rows, 2, head_width).transpose(1, 0, 2),
        ],
        axis=-1,
    )
    dense_w = jnp.stack(
        [
            w_up.reshape(d_rows, 2, units).transpose(1, 0, 2),
            w_down.T.reshape(d_rows, 2, units).transpose(1, 0, 2),
        ],
        axis=1,
    )

    def pair_up(parts, axis):
        mine = lax.dynamic_index_in_dim(parts, y, 0, keepdims=False)
        other = exchange(lax.dynamic_index_in_dim(parts, 1 - y, 0, keepdims=False), 1, 0)
        return halves_first(y, mine, other, axis)

    attend_full = gather_groups(pair_up(attend_w, 0)).reshape(d_model, 4 * head_width)
    x_rows = gather_rows(layer_in)
    dense_full = gather_groups(pair_up(dense_w, 1))
    up_full = dense_full[:, 0].reshape(d_model, units)
    down_full = dense_full[:, 1].reshape(d_model, units)
    g_rows = gather_rows(grad_out)
    qkv_full = attend_full[:, : 3 * head_width]
    out_full = attend_full[:, 3 * head_width :]

    positions = halves_first(y, doc_pos, exchange(doc_pos, 1, 0), 0)
    b_qkv_half = lax.dynamic_index_in_dim(b_qkv.reshape(2, -1), y, 0, keepdims=False)
    b_up_half = lax.dynamic_index_in_dim(b_up.reshape(2, -1), y, 0, keepdims=False)

    normed_rows, _ = normalize(x_rows.astype(F32))
    first_in = (normed_rows * gain_attend + shift_attend).astype(BF)
    second_in = (normed_rows * gain_dense + shift_dense).astype(BF)
    row_count = first_in.shape[0]

    joined_qkv = (dot_nn(first_in, qkv_full) + b_qkv_half).reshape(row_count, my_heads, 3, HD)
    cos_tab, sin_tab = rotary_tables(positions)
    cos_tab = cos_tab[:, None, :]
    sin_tab = sin_tab[:, None, :]
    queries = rotate(joined_qkv[:, :, 0], cos_tab, sin_tab).astype(BF)
    keys_rot = rotate(joined_qkv[:, :, 1], cos_tab, sin_tab).astype(BF)
    values = joined_qkv[:, :, 2].astype(BF)
    own_pair = jnp.concatenate(
        [keys_rot.reshape(row_count, head_width), values.reshape(row_count, head_width)], axis=1
    )
    reach = -(-(DOC_MAX - 1) // row_count)
    key_pairs = [own_pair]
    for _ in range(reach):
        key_pairs.append(shift_groups(key_pairs[-1], 1))

    preact = dot_nn(second_in, up_full) + b_up_half
    hidden = jax.nn.gelu(preact, approximate=False).astype(BF)
    dpreact = dot_nn(g_rows, down_full) * gelu_slope(preact)
    dpreact_b = dpreact.astype(BF)
    bup_part = jnp.sum(dpreact, axis=0)
    dense_grad = jnp.stack(
        [
            dot_tn(second_in, dpreact_b).reshape(-1, 2 * d_rows, units),
            dot_tn(g_rows, hidden).reshape(-1, 2 * d_rows, units),
        ],
        axis=1,
    )
    dense_own = scatter_groups(dense_grad)

    query_at = group * row_count + jnp.arange(row_count, dtype=jnp.int32)
    block_masks = []
    for distance in range(reach + 1):
        key_at = query_at - distance * row_count
        offsets = query_at[:, None] - key_at[None, :]
        block_masks.append(
            (offsets >= 0)
            & (offsets <= positions[:, None])
            & (query_at[:, None] // SEQ == key_at[None, :] // SEQ)
        )

    def split_pair(key_pair):
        return (
            key_pair[:, :head_width].reshape(row_count, my_heads, HD),
            key_pair[:, head_width:].reshape(row_count, my_heads, HD),
        )

    def block_scores(keys_blk, allowed):
        raw_scores = (
            jnp.einsum("qhd,khd->hqk", queries, keys_blk, preferred_element_type=F32) * score_scale
        )
        return jnp.where(allowed[None], raw_scores, MASKED)

    split_pairs = [split_pair(key_pair) for key_pair in key_pairs]
    all_scores = [
        block_scores(keys_blk, allowed)
        for (keys_blk, _), allowed in zip(split_pairs, block_masks)
    ]
    row_peak = all_scores[0].max(axis=-1)
    for scores in all_scores[1:]:
        row_peak = jnp.maximum(row_peak, scores.max(axis=-1))
    row_total = jnp.zeros_like(row_peak)
    for scores in all_scores:
        row_total = row_total + jnp.sum(jnp.exp(scores - row_peak[..., None]), axis=-1)
    logsum = row_peak + jnp.log(row_total)
    context = jnp.zeros((row_count, my_heads, HD), F32)
    for scores, (_, values_blk) in zip(all_scores, split_pairs):
        softmax = jnp.exp(scores - logsum[..., None]).astype(BF)
        context = context + jnp.einsum(
            "hqk,khd->qhd", softmax, values_blk, preferred_element_type=F32
        )
    context_b = context.reshape(row_count, head_width).astype(BF)

    branch = scatter_rows(dot_nt(context_b, out_full) + dot_nt(hidden, down_full))
    x_float = layer_in.astype(F32)
    layer_out = (x_float + b_out + b_down + branch).astype(BF)

    dcontext = dot_nn(g_rows, out_full).astype(BF)
    dctx_heads = dcontext.reshape(row_count, my_heads, HD)
    deltas = jnp.sum(
        dctx_heads.astype(F32) * context_b.reshape(row_count, my_heads, HD).astype(F32), axis=-1
    ).T
    dqueries = jnp.zeros((row_count, my_heads, HD), F32)
    pair_grads = []
    for (keys_blk, values_blk), allowed in zip(split_pairs, block_masks):
        scores = block_scores(keys_blk, allowed)
        softmax_f = jnp.exp(scores - logsum[..., None])
        softmax_b = softmax_f.astype(BF)
        dvalues = jnp.einsum("hqk,qhd->khd", softmax_b, dctx_heads, preferred_element_type=F32)
        dsoftmax = jnp.einsum("qhd,khd->hqk", dctx_heads, values_blk, preferred_element_type=F32)
        dscores = (softmax_f * (dsoftmax - deltas[..., None]) * score_scale).astype(BF)
        dqueries = dqueries + jnp.einsum(
            "hqk,khd->qhd", dscores, keys_blk, preferred_element_type=F32
        )
        dkeys = jnp.einsum("hqk,qhd->khd", dscores, queries, preferred_element_type=F32)
        pair_grads.append(
            jnp.concatenate(
                [dkeys.reshape(row_count, head_width), dvalues.reshape(row_count, head_width)],
                axis=1,
            )
        )
    pair_total = pair_grads[reach]
    for distance in range(reach - 1, -1, -1):
        pair_total = pair_grads[distance] + shift_groups(pair_total.astype(BF), -1).astype(F32)
    dq_pre = rotate_back(dqueries, cos_tab, sin_tab)
    dk_pre = rotate_back(
        pair_total[:, :head_width].reshape(row_count, my_heads, HD), cos_tab, sin_tab
    )
    dfused = jnp.stack(
        [dq_pre, dk_pre, pair_total[:, head_width:].reshape(row_count, my_heads, HD)], axis=2
    ).reshape(row_count, 3 * head_width)
    bqkv_part = jnp.sum(dfused, axis=0)
    dfused_b = dfused.astype(BF)

    attend_own = scatter_groups(
        jnp.concatenate([dot_tn(first_in, dfused_b), dot_tn(g_rows, context_b)], axis=1).reshape(
            -1, 2 * d_rows, 4 * head_width
        )
    )

    dfirst = dot_nt(dfused_b, qkv_full)
    dsecond = dot_nt(dpreact_b, up_full)
    dnormed = scatter_rows(dfirst * gain_attend + dsecond * gain_dense)
    normed, inv_std = normalize(x_float)
    grad_float = grad_out.astype(F32)
    grad_in = grad_float + norm_back(dnormed, normed, inv_std)

    width = max(d_model, 3 * head_width + units)
    columns = jnp.pad(
        jnp.concatenate([bqkv_part, bup_part]), (0, width - 3 * head_width - units)
    )
    sums = [
        jnp.sum(dfirst * normed_rows, axis=0),
        jnp.sum(dfirst, axis=0),
        jnp.sum(dsecond * normed_rows, axis=0),
        jnp.sum(dsecond, axis=0),
        jnp.sum(grad_float, axis=0),
    ]
    vectors = jnp.stack([jnp.pad(v, (0, width - d_model)) for v in sums] + [columns], axis=0)
    vectors = sum_groups(vectors)
    partner = exchange(vectors, 1, 0)
    col_mine, col_other = vectors[5], partner[5]
    db_qkv = halves_first(y, col_mine[: 3 * head_width], col_other[: 3 * head_width], 0)
    db_up = halves_first(
        y,
        col_mine[3 * head_width : 3 * head_width + units],
        col_other[3 * head_width : 3 * head_width + units],
        0,
    )
    vectors = (vectors + partner)[:5]
    vectors = vectors + exchange(vectors, 0, 2)
    vectors = (vectors + exchange(vectors, 0, 1))[:, :d_model]

    def settle(owned):
        parts = owned.reshape(owned.shape[:-2] + (2, d_rows, owned.shape[-1]))
        axis = parts.ndim - 3
        mine = lax.dynamic_index_in_dim(parts, y, axis, keepdims=False)
        sent = lax.dynamic_index_in_dim(parts, 1 - y, axis, keepdims=False).astype(BF)
        return mine, exchange(sent, 1, 0).astype(F32)

    dense_mine, dense_other = settle(dense_own)
    dw_up = halves_first(y, dense_mine[0], dense_other[0], 1)
    dw_down = halves_first(y, dense_mine[1], dense_other[1], 1).T
    attend_mine, attend_other = settle(attend_own)
    qkv_cols = 3 * head_width
    dw_qkv = halves_first(y, attend_mine[:, :qkv_cols], attend_other[:, :qkv_cols], 1)
    dw_out = halves_first(y, attend_mine[:, qkv_cols:], attend_other[:, qkv_cols:], 1).T
    return (
        layer_out,
        grad_in,
        vectors[0],
        vectors[1],
        vectors[2],
        vectors[3],
        dw_qkv,
        db_qkv,
        dw_out,
        vectors[4],
        dw_up,
        db_up,
        dw_down,
        vectors[4],
    )


def solution(mesh):
    return jax.shard_map(
        shards,
        mesh=mesh,
        in_specs=(
            P(("dp", "tensor"), None),
            P("dp"),
            P(),
            P(),
            P(),
            P(),
            P("dp", "tensor"),
            P("tensor"),
            P("tensor", "dp"),
            P(),
            P("dp", "tensor"),
            P("tensor"),
            P("tensor", "dp"),
            P(),
            P(("dp", "tensor"), None),
        ),
        out_specs=(
            P(("dp", "tensor"), None),
            P(("dp", "tensor"), None),
            P(),
            P(),
            P(),
            P(),
            P("dp", "tensor"),
            P("tensor"),
            P("tensor", "dp"),
            P(),
            P("dp", "tensor"),
            P("tensor"),
            P("tensor", "dp"),
            P(),
        ),
        check_vma=False,
    )
```

```python
import jax
import jax.numpy as jnp
import numpy as np
from jax import lax
from jax.experimental import pallas as pl
from jax.experimental.pallas import tpu as pltpu
from jax.sharding import PartitionSpec as P

HEADS = 16
HD = 64
ROT = 16
SEQ = 4096
DOC_MAX = 2000
EPS = 1e-05
MASKED = -1e30
SCALE = HD ** (-0.5)
TQ = 256
TK = 512
AXES = ("dp", "tensor")
BF = jnp.bfloat16
F32 = jnp.float32


def exchange(value, by_dp, by_tensor):
    tensor = lax.axis_size("tensor")
    count = lax.axis_size("dp") * tensor
    pairs = [
        (i, ((i // tensor) ^ by_dp) * tensor + ((i % tensor) ^ by_tensor)) for i in range(count)
    ]
    return lax.ppermute(value, AXES, pairs)


def shift_groups(value, by):
    count = lax.axis_size("dp")
    pairs = [(i, i + 2 * by) for i in range(count) if 0 <= i + 2 * by < count]
    return lax.ppermute(value, "dp", pairs)


def column_groups():
    return [[2 * g + y for g in range(lax.axis_size("dp") // 2)] for y in range(2)]


def group_count():
    return lax.axis_size("dp") // 2


def relative():
    return group_count() == 4


def order_scalars(rows):
    dp = lax.axis_index("dp")
    y = dp % 2
    own = dp % 8 if relative() else 0 * dp
    flip = (y * 4 + lax.axis_index("tensor")) * (rows // 8)
    seq_start = 2 * rows - ((dp // 2) * rows) % SEQ
    return jnp.stack([own, flip, seq_start]).astype(jnp.int32)


def pair_up(parts, axis):
    y = lax.axis_index("dp") % 2
    mine = lax.dynamic_index_in_dim(parts, y, 0, keepdims=False)
    other = exchange(lax.dynamic_index_in_dim(parts, 1 - y, 0, keepdims=False), 1, 0)
    if relative():
        return jnp.concatenate([mine, other], axis=axis)
    return halves_first(y, mine, other, axis)


def gather_groups(piece):
    if not relative():
        whole = lax.all_gather(piece, "dp", axis=0, axis_index_groups=column_groups())
        if whole.ndim == 4:
            whole = whole.transpose(1, 0, 2, 3)
            whole = whole.reshape(whole.shape[0], 4, -1, whole.shape[-1])
            return [whole[:, i] for i in range(4)]
        whole = whole.reshape(4, -1, whole.shape[-1])
        return [whole[i] for i in range(4)]
    near = exchange(piece, 2, 0)
    far = exchange(piece, 4, 0)
    return [piece, near, far, exchange(far, 2, 0)]


def scatter_groups(parts, d_rows):
    if not relative():
        whole = jnp.concatenate([p.astype(F32) for p in parts], axis=-2)
        groups = group_count()
        if whole.ndim == 3:
            whole = whole.reshape(whole.shape[0], groups, 2 * d_rows, -1).transpose(1, 0, 2, 3)
        else:
            whole = whole.reshape(groups, 2 * d_rows, -1)
        return lax.psum_scatter(
            whole, "dp", scatter_dimension=0, axis_index_groups=column_groups()
        )
    relayed = parts[2] + exchange(parts[3], 2, 0).astype(F32)
    near = exchange(parts[1], 2, 0).astype(F32)
    far = exchange(relayed.astype(BF), 4, 0).astype(F32)
    return parts[0] + near + far


def settle(owned, d_rows):
    y = lax.axis_index("dp") % 2
    axis = owned.ndim - 2
    if relative():
        mine = lax.slice_in_dim(owned, 0, d_rows, axis=axis)
        sent = lax.slice_in_dim(owned, d_rows, 2 * d_rows, axis=axis)
    else:
        mine = lax.dynamic_slice_in_dim(owned, y * d_rows, d_rows, axis=axis)
        sent = lax.dynamic_slice_in_dim(owned, (1 - y) * d_rows, d_rows, axis=axis)
    return mine, exchange(sent.astype(BF), 1, 0).astype(F32)


def sum_groups(vectors):
    if not relative():
        gathered = lax.all_gather(vectors, "dp", axis=0, axis_index_groups=column_groups())
        return jnp.sum(gathered, axis=0)
    vectors = vectors + exchange(vectors, 2, 0)
    return vectors + exchange(vectors, 4, 0)


def gather_rows(rows):
    near = [rows, exchange(rows, 0, 2), exchange(rows, 1, 0), exchange(rows, 1, 2)]
    blocks = []
    for piece in near:
        blocks += [piece, exchange(piece, 0, 1)]
    return blocks


def scatter_rows(kept, sent):
    four = kept + exchange(sent, 0, 1).astype(F32)
    return (
        four[0],
        exchange(four[1].astype(BF), 0, 2),
        exchange(four[2].astype(BF), 1, 0),
        exchange(four[3].astype(BF), 1, 2),
    )


def halves_first(y, mine, other, axis):
    return jnp.where(
        y == 0,
        jnp.concatenate([mine, other], axis=axis),
        jnp.concatenate([other, mine], axis=axis),
    )


def normalize(x_float):
    average = jnp.mean(x_float, axis=-1, keepdims=True)
    centred = x_float - average
    inv_std = lax.rsqrt(jnp.mean(centred * centred, axis=-1, keepdims=True) + EPS)
    return (centred * inv_std, inv_std)


def norm_back(dnormed, normed, inv_std):
    return inv_std * (
        dnormed
        - jnp.mean(dnormed, axis=-1, keepdims=True)
        - normed * jnp.mean(dnormed * normed, axis=-1, keepdims=True)
    )


def turn(vectors, cos_tab, sin_low, sin_high, sign):
    half_rot = ROT // 2
    width = vectors.shape[-1]
    ahead = pltpu.roll(vectors, width - half_rot, 1)
    behind = pltpu.roll(vectors, half_rot, 1)
    return vectors * cos_tab + sign * (behind * sin_high - ahead * sin_low)


def swap_blocks(value, active):
    if not active:
        return value
    count = value.shape[-1] // 128
    return jnp.concatenate(
        [value[:, (j ^ 1) * 128 : ((j ^ 1) + 1) * 128] for j in range(count)], axis=-1
    )


def lane_table():
    table = np.zeros((128, 3 * 128), np.float32)
    for lane in range(128):
        part = lane % HD
        if part >= ROT:
            table[2, lane] = 1.0
            continue
        i = part % (ROT // 2)
        table[16 + i, lane] = table[24 + i, lane] = 1.0
        at = 128 + lane if part < ROT // 2 else 256 + lane
        table[32 + i, at] = table[40 + i, at] = 1.0
    return jnp.asarray(table, BF)


def dot_nn(left, right):
    return jnp.dot(left, right, preferred_element_type=F32)


def dot_nt(left, right):
    return lax.dot_general(left, right, (((1,), (1,)), ((), ())), preferred_element_type=F32)


def dot_tn(left, right):
    return lax.dot_general(left, right, (((0,), (0,)), ((), ())), preferred_element_type=F32)


VMEM_SPEC = pl.BlockSpec(memory_space=pltpu.VMEM)
SMEM_SPEC = pl.BlockSpec(memory_space=pltpu.SMEM)


def whole_call(kernel, out, scalars, args, name, flops=0, moved=0, scratch=(), power=0):
    return pl.pallas_call(
        kernel,
        in_specs=[SMEM_SPEC] + [VMEM_SPEC] * len(args),
        out_specs=[VMEM_SPEC] * len(out),
        out_shape=[jax.ShapeDtypeStruct(s, t) for s, t in out],
        scratch_shapes=list(scratch),
        compiler_params=pltpu.CompilerParams(vmem_limit_bytes=48 * 2**20),
        cost_estimate=pl.CostEstimate(
            flops=flops, bytes_accessed=moved, transcendentals=power
        ),
        name=name,
    )(scalars, *args)


def prepare_kernel(
    scalars, x_ref, pos_ref, freq_ref, vec_ref, g_ref, xp_ref, gp_ref, rel_ref, gsum_ref
):
    own = scalars[0]
    depth = x_ref.shape[1]
    for j in range(depth // 128):
        at = pl.ds(pl.multiple_of((own ^ j) * 128, 128), 128)
        cols = slice(j * 128, (j + 1) * 128)
        xp_ref[:, cols] = x_ref[:, at]
        gp_ref[:, cols] = g_ref[:, at]
        rel_ref[:, cols] = vec_ref[:, at]
    pos = pos_ref[...]
    lane = lax.broadcasted_iota(jnp.int32, pos.shape, 1)
    angle = pos * freq_ref[...]
    cosine, sine = jnp.cos(angle), jnp.sin(angle)
    cos_high = cosine.astype(BF).astype(F32)
    sin_high = sine.astype(BF).astype(F32)
    upper = jnp.floor(pos * (1.0 / 64.0))
    side = jnp.where(lane == 0, upper, pos - 64.0 * upper)
    side = jnp.where(lane == 2, 1.0, side)
    side = jnp.where(lane >= 16, cos_high, side)
    side = jnp.where(lane >= 24, cosine - cos_high, side)
    side = jnp.where(lane >= 32, sin_high, side)
    side = jnp.where(lane >= 40, sine - sin_high, side)
    side = jnp.where(lane >= 48, 0.0, side)
    xp_ref[:, depth:] = side.astype(BF)
    gsum_ref[...] = jnp.sum(g_ref[...].astype(F32), axis=0, keepdims=True)


def front_kernel(swap, scalars, *refs):
    x_refs, w_refs = refs[:8], refs[8:12]
    vec_ref, bias_ref, lanes_ref, norm_ref, q_ref, kv_ref, tabs_ref, low_ref = refs[12:]
    width = q_ref.shape[1]
    depth = norm_ref.shape[1]
    rows = norm_ref.shape[0]
    pair = rows // 4
    flip, seq_start = scalars[1], scalars[2]
    for i in range(4):
        both = jnp.concatenate([x_refs[2 * i][...], x_refs[2 * i + 1][...]], axis=0)
        side = both[:, depth:]
        x = swap_blocks(both[:, :depth], swap and i >= 2).astype(F32)
        normed, _ = normalize(x)
        spot = slice(i * pair, (i + 1) * pair)
        norm_ref[spot, :] = normed
        first_in = (normed * vec_ref[0:1] + vec_ref[1:2]).astype(BF)
        quarter = depth // 4
        joined = bias_ref[...]
        for k in range(4):
            joined = joined + dot_nn(
                first_in[:, k * quarter : (k + 1) * quarter], w_refs[k][:, : 3 * width]
            )
        table = dot_nn(side, lanes_ref[...])
        tabs_ref[spot, :] = table
        tabs = (table[:, :width], table[:, width : 2 * width], table[:, 2 * width :])
        q_ref[spot, :] = turn(joined[:, :width], *tabs, 1.0).astype(BF)
        kv_ref[spot, :width] = turn(joined[:, width : 2 * width], *tabs, 1.0).astype(BF)
        kv_ref[spot, width:] = joined[:, 2 * width :].astype(BF)
        side_f = side.astype(F32)
        pos = side_f[:, 0:1] * 64.0 + side_f[:, 1:2]
        pos_row = jnp.broadcast_to(pos, (pair, 128)).T[0:1]
        place = (lax.broadcasted_iota(jnp.int32, (1, pair), 1) + i * pair) ^ flip
        low_ref[:, spot] = jnp.maximum(
            2 * rows + place - pos_row.astype(jnp.int32), seq_start
        )


def grads_kernel(swap, scalars, *refs):
    g_refs, w_refs = refs[:8], refs[8:12]
    rows_ref, dctx_ref = refs[12:]
    width = dctx_ref.shape[1]
    pair = rows_ref.shape[0] // 4
    quarter = rows_ref.shape[1] // 4
    for i in range(4):
        both = jnp.concatenate([g_refs[2 * i][...], g_refs[2 * i + 1][...]], axis=0)
        both = swap_blocks(both, swap and i >= 2)
        spot = slice(i * pair, (i + 1) * pair)
        rows_ref[spot, :] = both
        total = jnp.zeros((pair, width), F32)
        for k in range(4):
            total = total + dot_nn(
                both[:, k * quarter : (k + 1) * quarter], w_refs[k][:, 3 * width :]
            )
        dctx_ref[spot, :] = total.astype(BF)


def dense_kernel(scalars, *refs):
    norm_ref, g_ref = refs[:2]
    w_refs = refs[2:6]
    vec_ref, bias_ref, hidden_ref, dpre_ref, sum_ref = refs[6:11]
    part_refs, total = refs[11:15], refs[15]
    rows, depth = norm_ref.shape
    quarter = depth // 4
    sum_ref[...] = jnp.zeros_like(sum_ref)

    def tile(i, carry):
        spot = pl.ds(pl.multiple_of(i * TQ, TQ), TQ)
        second_in = (norm_ref[spot, :] * vec_ref[2:3] + vec_ref[3:4]).astype(BF)
        g = g_ref[spot, :]
        preact = bias_ref[...]
        dhidden = jnp.zeros((TQ, dpre_ref.shape[1]), F32)
        for k in range(4):
            cols = slice(k * quarter, (k + 1) * quarter)
            preact = preact + dot_nn(second_in[:, cols], w_refs[k][0])
            dhidden = dhidden + dot_nn(g[:, cols], w_refs[k][1])
        bell = 0.5 * (1.0 + lax.erf(preact * 0.7071067811865476))
        hidden = (preact * bell).astype(BF)
        slope = bell + preact * jnp.exp(-0.5 * preact * preact) * 0.3989422804014327
        dpre = dhidden * slope
        dpre_b = dpre.astype(BF)
        hidden_ref[spot, :] = hidden
        dpre_ref[spot, :] = dpre_b
        sum_ref[...] += jnp.sum(dpre, axis=0, keepdims=True)
        return carry

    lax.fori_loop(0, rows // TQ, tile, 0)
    dpre_all = dpre_ref[...]
    hidden_all = hidden_ref[...]

    def column(k):
        cols = slice(k * quarter, (k + 1) * quarter)
        second_in = (norm_ref[:, cols] * vec_ref[2:3, cols] + vec_ref[3:4, cols]).astype(BF)
        part_refs[k][0] = dot_tn(second_in, dpre_all).astype(part_refs[k].dtype)
        part_refs[k][1] = dot_tn(g_ref[:, cols], hidden_all).astype(part_refs[k].dtype)

    for k in range(4):
        column(k)


def branch_kernel(scalars, *refs):
    ctx_ref, hidden_ref = refs[:2]
    a_refs, w_refs = refs[2:6], refs[6:10]
    keep_ref, send_ref = refs[10:]
    width = ctx_ref.shape[1]
    rows = keep_ref.shape[1]
    quarter = keep_ref.shape[2] // 4
    for i in range(4):
        spot = slice(2 * i * rows, 2 * (i + 1) * rows)
        ctx, hidden = ctx_ref[spot, :], hidden_ref[spot, :]
        for k in range(4):
            cols = slice(k * quarter, (k + 1) * quarter)
            part = dot_nt(ctx, a_refs[k][:, 3 * width :]) + dot_nt(hidden, w_refs[k][1])
            keep_ref[i, :, cols] = part[:rows]
            send_ref[i, :, cols] = part[rows:].astype(BF)


def back_kernel(scalars, *refs):
    dq_ref, own_ref, recv_ref, tabs_ref, norm_ref, g_ref, ctx_ref, dpre_ref = refs[:8]
    a_refs, w_refs = refs[8:12], refs[12:16]
    vec_ref, keep_ref, send_ref, sums_ref, bsum_ref = refs[16:21]
    part_refs, fused = refs[21:25], refs[25]
    width = dq_ref.shape[1]
    rows = keep_ref.shape[1]
    quarter = keep_ref.shape[2] // 4
    sums_ref[...] = jnp.zeros_like(sums_ref)
    bsum = jnp.zeros((1, 3 * width), F32)
    for i in range(4):
        spot = slice(2 * i * rows, 2 * (i + 1) * rows)
        table = tabs_ref[spot, :]
        tabs = (table[:, :width], table[:, width : 2 * width], table[:, 2 * width :])
        total = own_ref[spot, :] + recv_ref[spot, :].astype(F32)
        dfused = jnp.concatenate(
            [
                turn(dq_ref[spot, :], *tabs, -1.0),
                turn(total[:, :width], *tabs, -1.0),
                total[:, width:],
            ],
            axis=1,
        )
        bsum = bsum + jnp.sum(dfused, axis=0, keepdims=True)
        dfused_b = dfused.astype(BF)
        fused[spot, :] = dfused_b
        dpre = dpre_ref[spot, :]
        for k in range(4):
            cols = slice(k * quarter, (k + 1) * quarter)
            normed = norm_ref[spot, cols]
            dfirst = dot_nt(dfused_b, a_refs[k][:, : 3 * width])
            dsecond = dot_nt(dpre, w_refs[k][0])
            sums_ref[0:1, cols] += jnp.sum(dfirst * normed, axis=0, keepdims=True)
            sums_ref[1:2, cols] += jnp.sum(dfirst, axis=0, keepdims=True)
            sums_ref[2:3, cols] += jnp.sum(dsecond * normed, axis=0, keepdims=True)
            sums_ref[3:4, cols] += jnp.sum(dsecond, axis=0, keepdims=True)
            part = dfirst * vec_ref[0:1, cols] + dsecond * vec_ref[2:3, cols]
            keep_ref[i, :, cols] = part[:rows]
            send_ref[i, :, cols] = part[rows:].astype(BF)
    bsum_ref[...] = bsum
    for k in range(4):
        cols = slice(k * quarter, (k + 1) * quarter)
        first_in = (norm_ref[:, cols] * vec_ref[0:1, cols] + vec_ref[1:2, cols]).astype(BF)
        kind = part_refs[k].dtype
        part_refs[k][:, : 3 * width] = dot_tn(first_in, fused[...]).astype(kind)
        part_refs[k][:, 3 * width :] = dot_tn(g_ref[:, cols], ctx_ref[...]).astype(kind)


def collect(swap, own, out_ref, pieces):
    first, by_x, by_y, by_xy = pieces
    total = first[...] + by_x[...].astype(F32)
    total = total + swap_blocks(by_y[...].astype(F32) + by_xy[...].astype(F32), swap)
    for j in range(total.shape[1] // 128):
        at = pl.ds(pl.multiple_of((own ^ j) * 128, 128), 128)
        out_ref[:, at] = total[:, j * 128 : (j + 1) * 128]


def finish_out_kernel(swap, scalars, *refs):
    x_ref, bias_ref, out_ref, total = refs[4:]
    collect(swap, scalars[0], total, refs[:4])
    out_ref[...] = (x_ref[...].astype(F32) + bias_ref[...] + total[...]).astype(BF)


def finish_grad_kernel(swap, scalars, *refs):
    x_ref, g_ref, out_ref, total = refs[4:]
    collect(swap, scalars[0], total, refs[:4])
    normed, inv_std = normalize(x_ref[...].astype(F32))
    out_ref[...] = g_ref[...].astype(F32) + norm_back(total[...], normed, inv_std)


def order_sums_kernel(scalars, sums_ref, out_ref):
    own = scalars[0]
    for j in range(sums_ref.shape[1] // 128):
        at = pl.ds(pl.multiple_of((own ^ j) * 128, 128), 128)
        out_ref[:, at] = sums_ref[:, j * 128 : (j + 1) * 128]


def attend_kernel(
    table,
    q_ref,
    far_ref,
    near_ref,
    own_ref,
    dctx_ref,
    low_ref,
    ctx_ref,
    dq_ref,
    dfar_ref,
    dnear_ref,
    down_ref,
    kv,
    kv_t,
    weights,
    dkv,
):
    rows, width = q_ref.shape
    heads = width // HD
    tiles = rows // TK
    flip = table[0]
    flip_tile = flip // TK
    inner_k = flip % TK
    inner_q = flip % TQ
    for i, ref in enumerate((far_ref, near_ref, own_ref)):
        kv[pl.ds(i * rows, rows), :] = ref[...]
        kv_t[:, pl.ds(i * rows, rows)] = ref[...].T
    dkv[...] = jnp.zeros_like(dkv)
    lane = lax.broadcasted_iota(jnp.int32, (1, width), 1) // HD
    key_iota = lax.broadcasted_iota(jnp.int32, (TK, TQ), 0) ^ inner_k
    query_iota = lax.broadcasted_iota(jnp.int32, (1, TQ), 1) ^ inner_q

    def place(tile):
        block = tile // tiles
        return pl.multiple_of((block * tiles + ((tile % tiles) ^ flip_tile)) * TK, TK)

    def per_query_tile(turn_q, carry):
        spot = pl.multiple_of((turn_q ^ (flip // TQ)) * TQ, TQ)
        q_tile = q_ref[pl.ds(spot, TQ), :].astype(F32) * SCALE
        dctx_tile = dctx_ref[pl.ds(spot, TQ), :].astype(F32)
        q_heads = [jnp.where(lane == h, q_tile, 0.0) for h in range(heads)]
        d_heads = [jnp.where(lane == h, dctx_tile, 0.0) for h in range(heads)]
        q_heads_t = [v.T.astype(BF) for v in q_heads]
        d_heads_t = [v.T.astype(BF) for v in d_heads]
        q_all = jnp.concatenate([v.astype(BF) for v in q_heads], axis=0)
        d_all = jnp.concatenate([v.astype(BF) for v in d_heads], axis=0)
        query_at = 2 * rows + turn_q * TQ + query_iota
        lowest = low_ref[:, pl.ds(spot, TQ)]
        first = jnp.min(lowest) // TK
        last = (2 * rows + turn_q * TQ + TQ - 1) // TK + 1

        def score(tile, peaks):
            keys = kv[pl.ds(place(tile), TK), :width]
            key_at = tile * TK + key_iota
            allowed = (key_at <= query_at) & (key_at >= lowest)
            found = []
            for h in range(heads):
                s = jnp.where(allowed, dot_nn(keys, q_heads_t[h]), MASKED)
                weights[h, pl.ds(tile * TK, TK), :] = s
                found.append(jnp.maximum(peaks[h], s.reshape(TK // 8, 8, TQ).max(axis=0)))
            return tuple(found)

        peaks = lax.fori_loop(
            first, last, score, tuple(jnp.full((8, TQ), MASKED, F32) for _ in range(heads))
        )
        peaks = [p.max(axis=0, keepdims=True) for p in peaks]

        def weigh(tile, state):
            values_t = kv_t[width:, pl.ds(place(tile), TK)]
            out = []
            for h in range(heads):
                total, context = state[h]
                p = jnp.exp(weights[h, pl.ds(tile * TK, TK), :] - peaks[h])
                weights[h, pl.ds(tile * TK, TK), :] = p
                out.append(
                    (
                        total + p.reshape(TK // 8, 8, TQ).sum(axis=0),
                        context + dot_nn(values_t[h * HD : (h + 1) * HD], p.astype(BF)),
                    )
                )
            return tuple(out)

        state = lax.fori_loop(
            first,
            last,
            weigh,
            tuple((jnp.zeros((8, TQ), F32), jnp.zeros((HD, TQ), F32)) for _ in range(heads)),
        )
        inverse = [1.0 / total.sum(axis=0, keepdims=True) for total, _ in state]
        context_t = jnp.concatenate([s[1] * inverse[h] for h, s in enumerate(state)], axis=0)
        context_b = context_t.T.astype(BF)
        ctx_ref[pl.ds(spot, TQ), :] = context_b
        product_t = dctx_tile.T * context_t.astype(BF).astype(F32)
        deltas = [
            product_t[h * HD : (h + 1) * HD].sum(axis=0, keepdims=True) for h in range(heads)
        ]

        def back(tile, dq_t):
            at = place(tile)
            keys_t = kv_t[:width, pl.ds(at, TK)]
            values = kv[pl.ds(at, TK), width:]
            ds_all, p_all, out = [], [], []
            for h in range(heads):
                soft = weights[h, pl.ds(tile * TK, TK), :] * inverse[h]
                dsoft = dot_nn(values, d_heads_t[h])
                ds = (soft * (dsoft - deltas[h])).astype(BF)
                ds_all.append(ds)
                p_all.append(soft.astype(BF))
                out.append(dq_t[h] + dot_nn(keys_t[h * HD : (h + 1) * HD], ds))
            dkv[pl.ds(at, TK), :width] += dot_nn(jnp.concatenate(ds_all, axis=1), q_all)
            dkv[pl.ds(at, TK), width:] += dot_nn(jnp.concatenate(p_all, axis=1), d_all)
            return tuple(out)

        dq_t = lax.fori_loop(
            first, last, back, tuple(jnp.zeros((HD, TQ), F32) for _ in range(heads))
        )
        dq_ref[pl.ds(spot, TQ), :] = jnp.concatenate(dq_t, axis=0).T * SCALE
        return carry

    lax.fori_loop(0, rows // TQ, per_query_tile, 0)
    dfar_ref[...] = dkv[pl.ds(0, rows), :].astype(BF)
    dnear_ref[...] = dkv[pl.ds(rows, rows), :]
    down_ref[...] = dkv[pl.ds(2 * rows, rows), :]


def attend(table, q, far, near, own, dctx, low):
    rows, width = q.shape
    heads = width // HD
    vmem = pl.BlockSpec(memory_space=pltpu.VMEM)
    pairs = rows * 2000 * heads
    return pl.pallas_call(
        attend_kernel,
        in_specs=[pl.BlockSpec(memory_space=pltpu.SMEM)] + [vmem] * 6,
        out_specs=[vmem] * 5,
        out_shape=[
            jax.ShapeDtypeStruct((rows, width), BF),
            jax.ShapeDtypeStruct((rows, width), F32),
            jax.ShapeDtypeStruct((rows, 2 * width), BF),
            jax.ShapeDtypeStruct((rows, 2 * width), F32),
            jax.ShapeDtypeStruct((rows, 2 * width), F32),
        ],
        scratch_shapes=[
            pltpu.VMEM((3 * rows, 2 * width), BF),
            pltpu.VMEM((2 * width, 3 * rows), BF),
            pltpu.VMEM((heads, 3 * rows, TQ), F32),
            pltpu.VMEM((3 * rows, 2 * width), F32),
        ],
        compiler_params=pltpu.CompilerParams(vmem_limit_bytes=40 * 2**20),
        cost_estimate=pl.CostEstimate(
            flops=14 * 4 * HD * pairs, bytes_accessed=16 * rows * width, transcendentals=pairs
        ),
        name="attend",
    )(table, q, far, near, own, dctx, low)


def shards(
    layer_in,
    doc_pos,
    gain_attend,
    shift_attend,
    gain_dense,
    shift_dense,
    w_qkv,
    b_qkv,
    w_out,
    b_out,
    w_up,
    b_up,
    w_down,
    b_down,
    grad_out,
):
    y = lax.axis_index("dp") % 2
    tensor = lax.axis_index("tensor")
    my_heads = HEADS // lax.axis_size("tensor") // 2
    width = my_heads * HD
    d_rows = w_qkv.shape[0]
    units = w_up.shape[1] // 2
    own_rows, depth = layer_in.shape
    rows = 8 * own_rows
    swap = relative()
    scalars = order_scalars(rows)

    def call(kernel, out, args, name, **kw):
        return whole_call(kernel, out, scalars, args, name, **kw)

    attend_w = jnp.concatenate(
        [
            w_qkv.reshape(d_rows, 2, my_heads, 3, HD)
            .transpose(1, 0, 3, 2, 4)
            .reshape(2, d_rows, 3 * width),
            w_out.T.reshape(d_rows, 2, width).transpose(1, 0, 2),
        ],
        axis=-1,
    )
    dense_w = jnp.stack(
        [
            w_up.reshape(d_rows, 2, units).transpose(1, 0, 2),
            w_down.T.reshape(d_rows, 2, units).transpose(1, 0, 2),
        ],
        axis=1,
    )
    own_pos = lax.dynamic_slice_in_dim(doc_pos, tensor * own_rows, own_rows).astype(F32)
    freq = jnp.power(10000.0, -2.0 * (jnp.arange(128, dtype=jnp.int32) % 8).astype(F32) / ROT)
    x_pack, g_pack, vec_rel, g_sum = call(
        prepare_kernel,
        [
            ((own_rows, depth + 128), BF),
            ((own_rows, depth), BF),
            ((4, depth), F32),
            ((1, depth), F32),
        ],
        [
            layer_in,
            jnp.broadcast_to(own_pos[:, None], (own_rows, 128)),
            freq[None],
            jnp.stack([gain_attend, shift_attend, gain_dense, shift_dense]),
            grad_out,
        ],
        "prepare",
        moved=2**20,
    )
    x_blocks = gather_rows(x_pack)
    attend_parts = gather_groups(pair_up(attend_w, 0))
    g_pack, dense_w, *_ = lax.optimization_barrier((g_pack, dense_w, x_blocks[6]))
    g_blocks = gather_rows(g_pack)
    dense_piece = pair_up(dense_w, 1)
    dense_piece, *_ = lax.optimization_barrier((dense_piece, attend_parts[2]))
    dense_parts = gather_groups(dense_piece)

    b_qkv_half = lax.dynamic_index_in_dim(b_qkv.reshape(2, -1), y, 0, keepdims=False)
    b_qkv_half = b_qkv_half.reshape(my_heads, 3, HD).transpose(1, 0, 2).reshape(1, 3 * width)
    b_up_half = lax.dynamic_index_in_dim(b_up.reshape(2, -1), y, 0)

    normed, queries, own_pair, tabs, low = call(
        lambda *r: front_kernel(swap, *r),
        [
            ((rows, depth), F32),
            ((rows, width), BF),
            ((rows, 2 * width), BF),
            ((rows, 3 * width), F32),
            ((1, rows), jnp.int32),
        ],
        [*x_blocks, *attend_parts, vec_rel, b_qkv_half, lane_table()],
        "front",
        flops=6 * rows * depth * width,
        moved=8 * rows * depth,
    )
    near_pair = shift_groups(own_pair, 1)
    far_pair = shift_groups(near_pair, 1)
    g_rows, dcontext = call(
        lambda *r: grads_kernel(swap, *r),
        [((rows, depth), BF), ((rows, width), BF)],
        [*g_blocks, *attend_parts],
        "grads",
        flops=2 * rows * depth * width,
        moved=4 * rows * depth,
    )
    piece = (2, depth // 4, units)
    hidden, dpre_b, bup_part, *dense_grads = call(
        dense_kernel,
        [
            ((rows, units), BF),
            ((rows, units), BF),
            ((1, units), F32),
            (piece, F32),
            (piece, BF),
            (piece, F32),
            (piece, BF),
        ],
        [normed, g_rows, *dense_parts, vec_rel, b_up_half],
        "dense",
        flops=8 * rows * depth * units,
        moved=10 * rows * depth,
        power=2 * rows * units,
        scratch=[pltpu.VMEM((8, 128), F32)],
    )
    context_b, dqueries, dfar, dnear, down_own = attend(
        scalars[1:2], queries, far_pair, near_pair, own_pair, dcontext, low
    )
    dnear = dnear + shift_groups(dfar, -1).astype(F32)
    recv = shift_groups(dnear.astype(BF), -1)
    dense_own = scatter_groups(dense_grads, d_rows)

    split = [((4, own_rows, depth), F32), ((4, own_rows, depth), BF)]
    branch = call(
        branch_kernel,
        split,
        [context_b, hidden, *attend_parts, *dense_parts],
        "branch",
        flops=2 * rows * depth * (units + width),
        moved=6 * rows * depth,
    )
    final = pltpu.VMEM((own_rows, depth), F32)
    (layer_out,) = call(
        lambda *r: finish_out_kernel(swap, *r),
        [((own_rows, depth), BF)],
        [*scatter_rows(*branch), layer_in, (b_out + b_down)[None]],
        "finish_out",
        moved=12 * own_rows * depth,
        scratch=[final],
    )
    piece = (depth // 4, 4 * width)
    kept, sent, sums, bqkv_part, *attend_grads = call(
        back_kernel,
        split
        + [
            ((4, depth), F32),
            ((1, 3 * width), F32),
            (piece, F32),
            (piece, BF),
            (piece, F32),
            (piece, BF),
        ],
        [
            dqueries,
            down_own,
            recv,
            tabs,
            normed,
            g_rows,
            context_b,
            dpre_b,
            *attend_parts,
            *dense_parts,
            vec_rel,
        ],
        "back",
        flops=2 * rows * depth * (units + 7 * width),
        moved=12 * rows * depth,
        scratch=[pltpu.VMEM((rows, 3 * width), BF)],
    )
    attend_own = scatter_groups(attend_grads, d_rows)
    (grad_in,) = call(
        lambda *r: finish_grad_kernel(swap, *r),
        [((own_rows, depth), F32)],
        [*scatter_rows(kept, sent), layer_in, grad_out],
        "finish_grad",
        moved=14 * own_rows * depth,
        scratch=[final],
    )
    (sums,) = call(order_sums_kernel, [((4, depth), F32)], [sums], "order_sums")

    span = max(depth, 3 * width + units)
    bqkv_part = bqkv_part.reshape(3, my_heads, HD).transpose(1, 0, 2).reshape(1, -1)
    columns = jnp.concatenate([bqkv_part, bup_part], axis=1)
    columns = jnp.pad(columns, ((0, 0), (0, span - 3 * width - units)))
    side = ((0, 0), (0, span - depth))
    vectors = jnp.concatenate([jnp.pad(sums, side), jnp.pad(g_sum, side), columns], axis=0)
    vectors = sum_groups(vectors)
    partner = exchange(vectors, 1, 0)
    col_mine, col_other = vectors[5], partner[5]
    db_qkv = halves_first(y, col_mine[: 3 * width], col_other[: 3 * width], 0)
    db_up = halves_first(
        y,
        col_mine[3 * width : 3 * width + units],
        col_other[3 * width : 3 * width + units],
        0,
    )
    vectors = (vectors + partner)[:5]
    vectors = vectors + exchange(vectors, 0, 2)
    vectors = (vectors + exchange(vectors, 0, 1))[:, :depth]

    dense_mine, dense_other = settle(dense_own, d_rows)
    dw_up = halves_first(y, dense_mine[0], dense_other[0], 1)
    dw_down = halves_first(y, dense_mine[1], dense_other[1], 1).T
    attend_mine, attend_other = settle(attend_own, d_rows)
    qkv_cols = 3 * width
    dw_qkv = halves_first(y, attend_mine[:, :qkv_cols], attend_other[:, :qkv_cols], 1)
    dw_qkv = (
        dw_qkv.reshape(d_rows, 2, 3, my_heads, HD).transpose(0, 1, 3, 2, 4).reshape(d_rows, -1)
    )
    dw_out = halves_first(y, attend_mine[:, qkv_cols:], attend_other[:, qkv_cols:], 1).T
    return (
        layer_out,
        grad_in,
        vectors[0],
        vectors[1],
        vectors[2],
        vectors[3],
        dw_qkv,
        db_qkv,
        dw_out,
        vectors[4],
        dw_up,
        db_up,
        dw_down,
        vectors[4],
    )


def solution(mesh):
    return jax.shard_map(
        shards,
        mesh=mesh,
        in_specs=(
            P(("dp", "tensor"), None),
            P("dp"),
            P(),
            P(),
            P(),
            P(),
            P("dp", "tensor"),
            P("tensor"),
            P("tensor", "dp"),
            P(),
            P("dp", "tensor"),
            P("tensor"),
            P("tensor", "dp"),
            P(),
            P(("dp", "tensor"), None),
        ),
        out_specs=(
            P(("dp", "tensor"), None),
            P(("dp", "tensor"), None),
            P(),
            P(),
            P(),
            P(),
            P("dp", "tensor"),
            P("tensor"),
            P("tensor", "dp"),
            P(),
            P("dp", "tensor"),
            P("tensor"),
            P("tensor", "dp"),
            P(),
        ),
        check_vma=False,
    )
```
